32 devices in a mesh: tm: 4 (over y, x), space: 8 (over z, core).
Axes of the slice: x: 2, y: 2, z: 4, core: 2. Of those that a mesh axis runs over, the one named last changes fastest.
Arguments:
- pixel_cot: bfloat16 [16, 64, 64, 128], P('tm', 'space'), may hold values from -6 to 6
- frame_group: int32 [16], P('tm'), may hold values from 0 to 3
- advantage: float32 [4], replicated, may hold values from -4 to 4
- block_in: bfloat16 [2, 16, 64, 64, 128], P(None, 'tm', 'space'), may hold values from -6 to 6
- conv1_weight: bfloat16 [2, 3, 3, 3, 128, 128], replicated, may hold values from -0.109375 to 0.109375
- conv2_weight: bfloat16 [2, 3, 3, 3, 128, 128], replicated, may hold values from -0.109375 to 0.109375
- owner_map: int32 [4, 8, 64, 1], P('tm', 'space'), may hold values from 0 to 7; in each aligned block of 64 rows (0 to 63, 64 to 127, ..., all dimensions but the last counted through in order) at most 16 rows name the same one
Outputs:
- latent_grad: bfloat16 [4, 8, 8, 16, 1024], P('tm', 'space')
The draws below stay inside these ranges and needn't reach their ends.
Inputs may be any that keep to these rules, and one draw needn't show every extreme that they name: `owner_map`: among the units of one device, at most 16 have the same owner, and in some devices exactly 16 do.
All inputs are finite; a program needn't handle non-finite values.
Results may differ from the reference program's by a relative error of at most 0.013.
Values may be sent and summed in bfloat16 or wider, within the bound.
A program may use at most 128 MiB of HBM per device.

```python
import math
import jax
import jax.numpy as jnp
import numpy as np
from jax import lax

CHAN = 128
BLOCKS = 2
GROUPS = 4
FRAME_DEV = 4
STRIP = 8
COLS = 64
FRAMES = 16
ROWS = 64
UNITS = 64
CAP = 16
N_TM = 4
N_SPACE = 8


def set_ends(drawn, rng, smallest, top_value):
    index_at = [jax.random.randint(jax.random.fold_in(rng, axis), (), 0, length) for axis, length in enumerate(drawn.shape)]
    longest = drawn.shape.index(max(drawn.shape))
    neighbour = index_at[:longest] + [(index_at[longest] + 1) % drawn.shape[longest]] + index_at[longest + 1:]
    return drawn.at[tuple(index_at)].set(smallest).at[tuple(neighbour)].set(top_value)


def block_scale(key, extent, shards, low, largest):
    level, own = 1.0, jax.random.fold_in(key, 6)
    for axis_at, parts in shards:
        steps = jnp.exp(jax.random.uniform(jax.random.fold_in(own, axis_at), (parts,), jnp.float32, low / len(shards), largest / len(shards)))
        level = level * jnp.repeat(steps, extent[axis_at] // parts).reshape([-1 if axis == axis_at else 1 for axis in range(len(extent))])
    return level


def routed_block(rng, own, number, rows, count, top, reach, lean):
    sequence = jax.random.permutation(rng, count)
    heavy_load, ordinary = portions_of(count, rows * top, reach, lean, True), portions_of(count, rows * top, reach, lean, False)
    places = jnp.arange(count)

    def named(lengths, offset_by):
        used = int((lengths > 0).sum())
        fixed = max(1, used // 4)
        passed = fixed + (places - fixed + offset_by * (used - fixed)) % max(1, count - fixed)
        return jnp.zeros((count,), jnp.int32).at[sequence[jnp.where(places < fixed, places, passed)]].set(jnp.asarray(lengths, jnp.int32))

    lengths = jnp.where(number % 4 == 0, named(heavy_load, number // 4), named(ordinary, number - number // 4 - 1))
    mixed = jax.random.permutation(jax.random.fold_in(own, 3), count)
    donor, receiver = mixed[0:count // 2 * 2:2], mixed[1:count // 2 * 2:2]
    slack = jnp.minimum(lengths[donor] - 1, reach - lengths[receiver]) // 2
    slack = jnp.where((donor == sequence[0]) | (receiver == sequence[0]) | (lengths[receiver] == 0), 0, jnp.maximum(slack, 0))
    passed = jax.random.randint(jax.random.fold_in(own, 4), (count // 2,), 0, 1 << 20) % (slack + 1)
    lengths = lengths.at[donor].add(-passed).at[receiver].add(passed)
    members = jnp.searchsorted(jnp.cumsum(lengths), jnp.arange(rows * top), side="right").astype(jnp.int32)
    grid = members.reshape(top, rows).T
    grid = grid[jax.random.permutation(jax.random.fold_in(own, 1), rows)]
    offset_by = jax.random.randint(jax.random.fold_in(own, 2), (rows, 1), 0, top)
    return jnp.take_along_axis(grid, (jnp.arange(top)[None, :] + offset_by) % top, axis=1)


def portions_of(amount, total, reach, slope, full):
    portions = [(1 << 20) // math.isqrt(standing ** slope) + 1 for standing in range(1, amount + 1)]
    largest = reach if full else min(reach, max(-(-total // amount), total * portions[0] // sum(portions)))
    least = 1 if total - largest >= amount - 1 else 0
    counts, rest = [largest] + [least] * (amount - 1), total - largest - least * (amount - 1)
    while rest > 0:
        candidates = [i for i in range(1, amount) if counts[i] < largest] or [i for i in range(1, amount) if counts[i] < reach]
        pool, remaining = sum([portions[i] for i in candidates]), rest
        for i in candidates:
            more = min(reach - counts[i], max(1, remaining * portions[i] // pool), rest)
            counts[i] = counts[i] + more
            rest = rest - more
    return np.array(counts)


def gaussian(stream_key, shape, scale, reach, cuts=(), kind=jnp.bfloat16):
    array = jax.random.normal(stream_key, shape, jnp.float32) * scale
    if len(cuts) > 0:
        array = block_scale(stream_key, shape, cuts, -0.22, 0.18) * array
    return jnp.clip(array, min=-reach, max=reach).astype(kind)


def setup_inputs(seed: int = 0) -> dict:
    key_list = jax.random.split(jax.random.key(seed), 8)
    pixel_cot = gaussian(key_list[0], (FRAMES, ROWS, COLS, CHAN), 1.0, 6.0, ((0, 4), (1, 8)))
    frame_group = set_ends(jax.random.randint(key_list[1], (FRAMES,), 0, GROUPS), jax.random.fold_in(key_list[1], 1), 0, GROUPS - 1).astype(jnp.int32)
    advantage = gaussian(key_list[2], (GROUPS,), 1.0, 4.0, (), jnp.float32)
    block_in = gaussian(key_list[3], (BLOCKS, FRAMES, ROWS, COLS, CHAN), 1.0, 6.0, ((1, 4), (2, 8)))
    conv1_weight = gaussian(key_list[4], (BLOCKS, 3, 3, 3, CHAN, CHAN), (27 * CHAN) ** -0.5, 0.109375)
    conv2_weight = gaussian(key_list[5], (BLOCKS, 3, 3, 3, CHAN, CHAN), (27 * CHAN) ** -0.5, 0.109375)
    owner_map_keys = jax.random.split(jax.random.fold_in(key_list[6], 1), N_TM * N_SPACE * UNITS // UNITS)
    owner_map_turns = jax.random.permutation(jax.random.fold_in(key_list[6], 3), N_TM * N_SPACE * UNITS // UNITS)
    owner_map = jax.vmap(lambda own, number: routed_block(jax.random.fold_in(key_list[6], 2), own, number, UNITS, N_SPACE, 1, CAP, 1))(owner_map_keys, owner_map_turns).reshape((N_TM, N_SPACE, UNITS, 1))
    return {"pixel_cot": pixel_cot, "frame_group": frame_group, "advantage": advantage, "block_in": block_in, "conv1_weight": conv1_weight, "conv2_weight": conv2_weight, "owner_map": owner_map}


def conv_forward(field, kernel):
    return lax.conv_general_dilated(field[None], kernel, (1, 1, 1), ((2, 0), (1, 1), (1, 1)), dimension_numbers=("NDHWC", "DHWIO", "NDHWC"), precision=lax.Precision.HIGHEST)[0]


def conv_backward(field, kernel):
    flipped = jnp.swapaxes(jnp.flip(kernel, (0, 1, 2)), 3, 4)
    return lax.conv_general_dilated(field[None], flipped, (1, 1, 1), ((0, 2), (1, 1), (1, 1)), dimension_numbers=("NDHWC", "DHWIO", "NDHWC"), precision=lax.Precision.HIGHEST)[0]


def reference(pixel_cot, frame_group, advantage, block_in, conv1_weight, conv2_weight, owner_map):
    frame_scale = advantage[frame_group]
    upstream = (pixel_cot.astype(jnp.float32) * frame_scale[:, None, None, None]).astype(jnp.bfloat16)
    for layer in reversed(range(BLOCKS)):
        inputs = block_in[layer].astype(jnp.float32)
        hidden_pre = conv_forward(inputs, conv1_weight[layer].astype(jnp.float32))
        grad_act = conv_backward(upstream.astype(jnp.float32), conv2_weight[layer].astype(jnp.float32))
        sigma = jax.nn.sigmoid(hidden_pre)
        grad_pre = (grad_act * (sigma * (1.0 + hidden_pre * (1.0 - sigma)))).astype(jnp.bfloat16)
        back = conv_backward(grad_pre.astype(jnp.float32), conv1_weight[layer].astype(jnp.float32))
        upstream = (upstream.astype(jnp.float32) + back).astype(jnp.bfloat16)
    pooled = upstream.astype(jnp.float32).reshape(FRAMES, ROWS // 2, 2, COLS // 2, 2, CHAN).sum(axis=(2, 4)).astype(jnp.bfloat16)
    units = pooled.reshape(N_TM, FRAME_DEV, N_SPACE, STRIP // 2, COLS // 16, 8 * CHAN)
    units = units.transpose(0, 2, 1, 3, 4, 5).reshape(N_TM, N_SPACE, UNITS, 8 * CHAN)
    owners = owner_map[..., 0]
    one_hot = (owners[..., None] == jnp.arange(N_SPACE, dtype=jnp.int32)).astype(jnp.int32)
    before = jnp.cumsum(one_hot, axis=2)
    position = jnp.sum(before * one_hot, axis=-1) - 1
    slot_index = owners * CAP + position
    placing = (slot_index[..., None, :] == jnp.arange(N_SPACE * CAP, dtype=jnp.int32)[:, None]).astype(jnp.float32)
    outgoing = jnp.einsum("abpu,abuk->abpk", placing, units.astype(jnp.float32), precision=lax.Precision.HIGHEST)
    outgoing = outgoing.astype(jnp.bfloat16).reshape(N_TM, N_SPACE, N_SPACE, CAP, 8 * CHAN)
    return outgoing.transpose(0, 2, 1, 3, 4)
```

```python
import functools

import jax
import jax.numpy as jnp
from jax import lax
from jax.experimental import pallas as pl
from jax.experimental.pallas import tpu as pltpu
from jax.sharding import PartitionSpec as P

F32 = jnp.float32
BF16 = jnp.bfloat16


def kernel(
    cot, group, adv, block_in, w1_hbm, w2_hbm, owner, out,
    w1, w2, fields, x_past, x_up, x_gr, pre_acc, grad_acc, pool_a, pool_b, outgoing,
    send_sem, recv_sem, a2a_send, a2a_recv, local_sem,
):
    frames, rows, cols, chan = cot.shape
    blocks = block_in.shape[0]
    pairs = frames // 2
    pixels = rows * cols
    n_tm, n_sp = lax.axis_size("tm"), lax.axis_size("space")
    tm, sp = lax.axis_index("tm"), lax.axis_index("space")
    yes = tm >= 0

    def up_field(layer):
        return blocks + 2 * layer

    def gr_field(layer):
        return blocks + 2 * layer + 1

    low, high = sp > 0, sp < n_sp - 1
    before, after = tm > 0, tm < n_tm - 1

    def remote(src, dst, field, channel, dtm, dsp):
        return pltpu.make_async_remote_copy(
            src_ref=src, dst_ref=dst,
            send_sem=send_sem.at[field, channel], recv_sem=recv_sem.at[field, channel],
            device_id={"tm": tm + dtm, "space": sp + dsp},
            device_id_type=pl.DeviceIdType.MESH,
        )

    def time_copies(field, past):
        buf = fields.at[field]
        if past:
            src = lambda r, n: block_in.at[field, frames - 2 : frames, r : r + n]
            dst = lambda r, n: buf.at[0:2, r : r + n]
            d, can, get = 1, after, before
        else:
            src = lambda r, n: buf.at[0:2, r + 1 : r + 1 + n]
            dst = lambda r, n: buf.at[frames : frames + 2, r : r + n]
            d, can, get = -1, before, after
        return [
            (remote(src(0, rows), dst(1, rows), field, 0, d, 0), can, get),
            (remote(src(0, 1), dst(rows + 1, 1), field, 1, d, -1), can & low, get & high),
            (remote(src(rows - 1, 1), dst(0, 1), field, 2, d, 1), can & high, get & low),
        ]

    def row_copies(field, past, pair):
        buf = fields.at[field]
        if past:
            src = lambda r: block_in.at[field, 2 * pair : 2 * pair + 2, r : r + 1]
            dst = lambda r: buf.at[2 + 2 * pair : 4 + 2 * pair, r : r + 1]
        else:
            src = lambda r: buf.at[2 * pair : 2 * pair + 2, r + 1 : r + 2]
            dst = lambda r: buf.at[2 * pair : 2 * pair + 2, r : r + 1]
        return [
            (remote(src(0), dst(rows + 1), field, 3 + 2 * pair, 0, -1), low, high),
            (remote(src(rows - 1), dst(0), field, 4 + 2 * pair, 0, 1), high, low),
        ]

    def start(copies):
        for copy, sends, _ in copies:
            pl.when(sends)(copy.start)

    def arrive(copies):
        for copy, _, gets in copies:
            pl.when(gets)(copy.wait_recv)

    def sent(copies):
        for copy, sends, _ in copies:
            pl.when(sends)(copy.wait_send)

    loads = {}

    def load(name, src, dst, number):
        loads[name] = pltpu.make_async_copy(src, dst, local_sem.at[number])
        loads[name].start()

    last = blocks - 1
    load("cot", cot, fields.at[up_field(last), 0:frames, 1 : rows + 1], 0)
    for layer in reversed(range(blocks)):
        load(("in", layer), block_in.at[layer], fields.at[layer, 2 : frames + 2, 1 : rows + 1], 1 + layer)
        load(("w1", layer), w1_hbm.at[layer], w1.at[layer], 1 + blocks + layer)
        load(("w2", layer), w2_hbm.at[layer], w2.at[layer], 1 + 2 * blocks + layer)

    barrier = pltpu.get_barrier_semaphore()

    def greet(dtm, to):
        pl.semaphore_signal(
            barrier, inc=1, device_id={"tm": tm + dtm, "space": to},
            device_id_type=pl.DeviceIdType.MESH,
        )

    for k in range(1, n_sp):
        greet(0, lax.rem(sp + k, n_sp))
    expected = n_sp - 1
    for dtm, can in ((1, after), (-1, before)):
        for dsp, there in ((0, yes), (-1, low), (1, high)):
            pl.when(can & there)(functools.partial(greet, dtm, sp + dsp))
            expected = expected + jnp.where(can & there, 1, 0)
    pl.semaphore_wait(barrier, expected)

    pair_range = range(pairs)
    start(row_copies(last, True, pairs - 1))
    for pair in reversed(range(pairs - 1)):
        start(row_copies(last, True, pair))
    start(time_copies(last, True))

    at_col = lax.broadcasted_iota(jnp.int32, (cols, chan), 0)

    def spread(x, frame, row, value):
        wide = value.astype(F32)
        left = jnp.where(at_col == 0, 0.0, pltpu.roll(wide, 1, axis=0))
        right = jnp.where(at_col == cols - 1, 0.0, pltpu.roll(wide, cols - 1, axis=0))
        x[frame, row, :, 0:chan] = left.astype(BF16)
        x[frame, row, :, chan : 2 * chan] = value
        x[frame, row, :, 2 * chan : 3 * chan] = right.astype(BF16)

    def clear(x, frame, row):
        x[frame, row] = jnp.zeros((cols, 3 * chan), BF16)

    def edge(x, field, frame, row, present):
        @pl.when(present)
        def _():
            spread(x, frame, row, fields[field, frame, row])

        @pl.when(jnp.logical_not(present))
        def _():
            clear(x, frame, row)

    def row_edges(x, field, past, pair):
        arrive(row_copies(field, past, pair))
        for i in range(2):
            frame = 2 * pair + i + (2 if past else 0)
            edge(x, field, frame, 0, low)
            edge(x, field, frame, rows + 1, high)

    def time_edges(x, field, past):
        arrive(time_copies(field, past))
        present = before if past else after
        for i in range(2):
            frame = i if past else frames + i

            @pl.when(present)
            def _():
                @pl.loop(1, rows + 1)
                def _(row):
                    spread(x, frame, row, fields[field, frame, row])

            @pl.when(jnp.logical_not(present))
            def _():
                @pl.loop(1, rows + 1)
                def _(row):
                    clear(x, frame, row)

            edge(x, field, frame, 0, present & low)
            edge(x, field, frame, rows + 1, present & high)

    def own_rows(x, field, past):
        @pl.loop(0, frames * rows)
        def _(at):
            frame = at // rows + (2 if past else 0)
            row = at % rows + 1
            spread(x, frame, row, fields[field, frame, row])

    def tap(w, layer, a, flip):
        if not flip:
            return w[layer, a].reshape(9 * chan, chan)
        return jnp.concatenate([w[layer, a, 2 - r, 2 - s] for r in range(3) for s in range(3)], axis=1)

    def conv(acc, x, w, layer, flip, pair, order, hooks):
        zero = jnp.zeros((chan, 9 * chan) if flip else (9 * chan, chan), BF16)
        outer = 0 if flip else 1

        def part(j, r, half):
            first = r + half * rows // 2
            return x[2 * pair + j, first : first + rows // 2].reshape(pixels // 2, 3 * chan)

        for step, group_of in enumerate(order):
            rhs = []
            for j in group_of:
                if j in hooks:
                    hooks[j]()
            for j in group_of:
                taps = [(2 - k if flip else k) if 0 <= k <= 2 else None for k in (j, j - 1)]
                parts = [zero if a is None else tap(w, layer, a, flip) for a in taps]
                rhs.append(jnp.concatenate(parts, axis=outer))
            right = jnp.concatenate(rhs, axis=1 if flip else 0)
            dims = (((1,), (1,)), ((), ())) if flip else (((1,), (0,)), ((), ()))
            for half in range(2):
                at = slice(half * pixels // 2, (half + 1) * pixels // 2)
                left = jnp.concatenate([part(j, r, half) for j in group_of for r in range(3)], axis=1)
                value = lax.dot_general(left, right, dims, preferred_element_type=F32)
                if step == 0:
                    acc[at] = value
                else:
                    acc[at] += value

    def conv_past(layer, pair):
        order, hooks = ((0, 1), (2, 3)), {}
        if pair == 0:
            order, hooks = ((2, 3), (0, 1)), {0: lambda: time_edges(x_past, layer, True)}
        conv(pre_acc.at[layer, pair], x_past, w1, layer, False, pair, order, hooks)

    def conv_future(x, w, layer, field, pair):
        hooks = {}
        if pair == 0:
            hooks[0] = lambda: row_edges(x, field, False, 0)
        if pair < pairs - 1:
            hooks[2] = lambda: row_edges(x, field, False, pair + 1)
        else:
            hooks[2] = lambda: time_edges(x, field, False)
        conv(grad_acc.at[pair], x, w, layer, True, pair, ((0, 1), (2, 3)), hooks)

    def send(field, pair):
        if pair == 0:
            start(time_copies(field, False))
        start(row_copies(field, False, pair))

    loads["cot"].wait()
    for frame in range(frames):
        scale = adv[group[frame]]

        @pl.loop(1, rows + 1)
        def _(row):
            value = (fields[up_field(last), frame, row].astype(F32) * scale).astype(BF16)
            fields[up_field(last), frame, row] = value
            spread(x_up, frame, row, value)

        if frame % 2 == 1:
            send(up_field(last), frame // 2)

    def grad_pre(layer, pair):
        field = gr_field(layer)
        for i in range(2):
            @pl.loop(0, rows)
            def _(row):
                at = pl.ds(pl.multiple_of(row * cols, cols), cols)
                lanes = slice(i * chan, (i + 1) * chan)
                grad = grad_acc[pair, at, lanes]
                pre = pre_acc[layer, pair, at, lanes]
                s = jax.nn.sigmoid(pre)
                value = (grad * (s * (1.0 + pre * (1.0 - s)))).astype(BF16)
                fields[field, 2 * pair + i, row + 1] = value
                spread(x_gr, 2 * pair + i, row + 1, value)
        send(field, pair)

    def next_up(layer, pair):
        field = up_field(layer - 1)
        for i in range(2):
            @pl.loop(0, rows)
            def _(row):
                at = pl.ds(pl.multiple_of(row * cols, cols), cols)
                back = grad_acc[pair, at, i * chan : (i + 1) * chan]
                value = (fields[up_field(layer), 2 * pair + i, row + 1].astype(F32) + back).astype(BF16)
                fields[field, 2 * pair + i, row + 1] = value
                spread(x_up, 2 * pair + i, row + 1, value)
        send(field, pair)

    def pool(layer, pair):
        for i in range(2):
            @pl.loop(0, rows // 2)
            def _(r):
                total = jnp.zeros((cols, chan), F32)
                for k in range(2):
                    row = 2 * r + k
                    at = pl.ds(pl.multiple_of(row * cols, cols), cols)
                    back = grad_acc[pair, at, i * chan : (i + 1) * chan]
                    value = fields[up_field(layer), 2 * pair + i, row + 1].astype(F32) + back
                    total = total + value.astype(BF16).astype(F32)
                at = pl.multiple_of(((2 * pair + i) * (rows // 2) + r) * cols, cols)
                pool_a[pl.ds(at, cols), :] = total

    def load_block(layer):
        loads[("in", layer)].wait()
        own_rows(x_past, layer, True)
        for pair in reversed(pair_range):
            row_edges(x_past, layer, True, pair)

    for layer in reversed(range(blocks)):
        up, gr = up_field(layer), gr_field(layer)
        if layer == last:
            load_block(layer)
            loads[("w1", layer)].wait()
            for pair in reversed(range(1, pairs)):
                conv_past(layer, pair)
        loads[("w2", layer)].wait()
        conv_future(x_up, w2, layer, up, 0)
        if layer == last:
            conv_past(layer, 0)
            for nxt in reversed(range(last)):
                for pair in reversed(pair_range):
                    start(row_copies(nxt, True, pair))
                start(time_copies(nxt, True))
        grad_pre(layer, 0)
        for pair in range(1, pairs):
            conv_future(x_up, w2, layer, up, pair)
            grad_pre(layer, pair)
        if layer > 0:
            load_block(layer - 1)
            loads[("w1", layer - 1)].wait()
            for pair in reversed(pair_range):
                conv_past(layer - 1, pair)
        for pair in pair_range:
            conv_future(x_gr, w1, layer, gr, pair)
            if layer > 0:
                next_up(layer, pair)
            else:
                pool(layer, pair)

    units_n = owner.shape[1]
    cap = out.shape[3]
    places = n_sp * cap
    lat = pool_b.shape[0]
    even = pool_a[pl.ds(0, lat, stride=2), :]
    odd = pool_a[pl.ds(1, lat, stride=2), :]
    pool_b[...] = (even + odd).astype(BF16).astype(F32)
    wide = lat // units_n
    units = jnp.concatenate(
        [pool_b[pl.ds(k, units_n, stride=wide), :] for k in range(wide)], axis=1
    ).astype(BF16)
    owners = owner[...]
    hot = jnp.where(owners == lax.broadcasted_iota(jnp.int32, (128, units_n), 0), 1.0, 0.0)
    tri = jnp.where(
        lax.broadcasted_iota(jnp.int32, (units_n, units_n), 0)
        <= lax.broadcasted_iota(jnp.int32, (units_n, units_n), 1), 1.0, 0.0,
    )
    ranks = jnp.dot(hot.astype(BF16), tri.astype(BF16), preferred_element_type=F32)
    position = jnp.sum(ranks * hot, axis=0, keepdims=True) - 1.0
    slot = owners.astype(F32) * cap + position
    chosen = jnp.where(
        slot == lax.broadcasted_iota(jnp.int32, (places, units_n), 0).astype(F32), 1.0, 0.0
    )
    placed = jnp.dot(chosen.astype(BF16), units, preferred_element_type=F32)
    for o in range(n_sp):
        outgoing[o] = placed[o * cap : (o + 1) * cap].astype(BF16)

    mine = pltpu.make_async_copy(outgoing.at[sp], out.at[0, 0, sp], local_sem.at[1 + 3 * blocks])
    mine.start()
    moves = []
    for k in range(1, n_sp):
        to = lax.rem(sp + k, n_sp)
        copy = pltpu.make_async_remote_copy(
            src_ref=outgoing.at[to], dst_ref=out.at[0, 0, sp],
            send_sem=a2a_send.at[k], recv_sem=a2a_recv.at[k],
            device_id={"space": to}, device_id_type=pl.DeviceIdType.MESH,
        )
        copy.start()
        moves.append(copy)
    mine.wait()
    for k, copy in enumerate(moves, 1):
        copy.wait_send()
        came = lax.rem(sp - k + n_sp, n_sp)
        pltpu.make_async_remote_copy(
            src_ref=outgoing.at[came], dst_ref=out.at[0, 0, came],
            send_sem=a2a_send.at[k], recv_sem=a2a_recv.at[k],
            device_id={"space": came}, device_id_type=pl.DeviceIdType.MESH,
        ).wait_recv()
    for layer in range(blocks):
        sent(time_copies(layer, True))
        for field in (up_field(layer), gr_field(layer)):
            sent(time_copies(field, False))
        for pair in pair_range:
            sent(row_copies(layer, True, pair))
            for field in (up_field(layer), gr_field(layer)):
                sent(row_copies(field, False, pair))


def on_device(pixel_cot, frame_group, advantage, block_in, conv1_weight, conv2_weight, owner_map):
    frames, rows, cols, chan = pixel_cot.shape
    blocks = block_in.shape[0]
    pairs = frames // 2
    units = owner_map.shape[2]
    n_sp = lax.axis_size("space")
    cap = max(2, 2 * units // n_sp)
    unit = frames * (rows // 2) * (cols // 2) * chan // units
    lat = frames * (rows // 2) * (cols // 2)
    spread = (frames + 2, rows + 2, cols, 3 * chan)
    smem = pl.BlockSpec(memory_space=pltpu.SMEM)
    hbm = pl.BlockSpec(memory_space=pl.ANY)
    vmem = pl.BlockSpec(memory_space=pltpu.VMEM)
    return pl.pallas_call(
        kernel,
        out_shape=jax.ShapeDtypeStruct((1, 1, n_sp, cap, unit), BF16),
        in_specs=[hbm, smem, smem, hbm, hbm, hbm, vmem],
        out_specs=hbm,
        scratch_shapes=[
            pltpu.VMEM(conv1_weight.shape, BF16),
            pltpu.VMEM(conv2_weight.shape, BF16),
            pltpu.VMEM((3 * blocks, frames + 2, rows + 2, cols, chan), BF16),
            pltpu.VMEM(spread, BF16),
            pltpu.VMEM(spread, BF16),
            pltpu.VMEM(spread, BF16),
            pltpu.VMEM((blocks, pairs, rows * cols, 2 * chan), F32),
            pltpu.VMEM((pairs, rows * cols, 2 * chan), F32),
            pltpu.VMEM((2 * lat, chan), F32),
            pltpu.VMEM((lat, chan), F32),
            pltpu.VMEM((n_sp, cap, unit), BF16),
            pltpu.SemaphoreType.DMA((3 * blocks, 3 + 2 * pairs)),
            pltpu.SemaphoreType.DMA((3 * blocks, 3 + 2 * pairs)),
            pltpu.SemaphoreType.DMA((n_sp,)),
            pltpu.SemaphoreType.DMA((n_sp,)),
            pltpu.SemaphoreType.DMA((2 + 3 * blocks,)),
        ],
        compiler_params=pltpu.CompilerParams(
            has_side_effects=True, collective_id=0, vmem_limit_bytes=60 * 1024 * 1024
        ),
    )(pixel_cot, frame_group, advantage, block_in, conv1_weight, conv2_weight, owner_map.reshape(1, units))


def solution(mesh):
    in_specs = (
        P("tm", "space", None, None),
        P("tm"),
        P(),
        P(None, "tm", "space", None, None),
        P(),
        P(),
        P("tm", "space", None, None),
    )
    out_specs = P("tm", "space", None, None, None)
    return jax.shard_map(
        on_device, mesh=mesh, in_specs=in_specs, out_specs=out_specs, check_vma=False
    )
```

```python
import functools

import jax
import jax.numpy as jnp
from jax import lax
from jax.experimental import pallas as pl
from jax.experimental.pallas import tpu as pltpu
from jax.sharding import PartitionSpec as P

F32 = jnp.float32
BF16 = jnp.bfloat16


def kernel(
    cot, group, adv, block_in, w1_hbm, w2_hbm, owner, out,
    w1, w2, fields, x_past, x_up, x_gr, pre_acc, grad_acc, pool_a, pool_b, outgoing,
    send_sem, recv_sem, a2a_send, a2a_recv, local_sem,
):
    frames, rows, cols, chan = cot.shape
    blocks = block_in.shape[0]
    pairs = frames // 2
    pixels = rows * cols
    n_tm, n_sp = lax.axis_size("tm"), lax.axis_size("space")
    tm, sp = lax.axis_index("tm"), lax.axis_index("space")

    def up_field(layer):
        return blocks + 2 * layer

    def gr_field(layer):
        return blocks + 2 * layer + 1

    low, high = sp > 0, sp < n_sp - 1
    before, after = tm > 0, tm < n_tm - 1

    def remote(src, dst, field, channel, dtm, dsp):
        return pltpu.make_async_remote_copy(
            src_ref=src, dst_ref=dst,
            send_sem=send_sem.at[field, channel], recv_sem=recv_sem.at[field, channel],
            device_id={"tm": tm + dtm, "space": sp + dsp},
            device_id_type=pl.DeviceIdType.MESH,
        )

    def time_copies(field, past):
        buf = fields.at[field]
        if past:
            src = lambda r, n: block_in.at[field, frames - 2 : frames, r : r + n]
            dst = lambda r, n: buf.at[0:2, r : r + n]
            d, can, get = 1, after, before
        else:
            src = lambda r, n: buf.at[0:2, r + 1 : r + 1 + n]
            dst = lambda r, n: buf.at[frames : frames + 2, r : r + n]
            d, can, get = -1, before, after
        return [(remote(src(0, rows), dst(1, rows), field, 0, d, 0), can, get)]

    def corner_copies(field, past):
        halo = fields.at[field, 0:2] if past else fields.at[field, frames : frames + 2]
        here = before if past else after
        row = lambda r: halo.at[:, r : r + 1]
        return [
            (remote(row(1), row(rows + 1), field, 1, 0, -1), here & low, here & high),
            (remote(row(rows), row(0), field, 2, 0, 1), here & high, here & low),
        ]

    def row_copies(field, past, pair):
        buf = fields.at[field]
        if past:
            src = lambda r: block_in.at[field, 2 * pair : 2 * pair + 2, r : r + 1]
            dst = lambda r: buf.at[2 + 2 * pair : 4 + 2 * pair, r : r + 1]
        else:
            src = lambda r: buf.at[2 * pair : 2 * pair + 2, r + 1 : r + 2]
            dst = lambda r: buf.at[2 * pair : 2 * pair + 2, r : r + 1]
        return [
            (remote(src(0), dst(rows + 1), field, 3 + 2 * pair, 0, -1), low, high),
            (remote(src(rows - 1), dst(0), field, 4 + 2 * pair, 0, 1), high, low),
        ]

    def start(copies):
        for copy, sends, _ in copies:
            pl.when(sends)(copy.start)

    def arrive(copies):
        for copy, _, gets in copies:
            pl.when(gets)(copy.wait_recv)

    def sent(copies):
        for copy, sends, _ in copies:
            pl.when(sends)(copy.wait_send)

    loads = {}

    def load(name, src, dst, number):
        loads[name] = pltpu.make_async_copy(src, dst, local_sem.at[number])
        loads[name].start()

    last = blocks - 1
    load("cot", cot, fields.at[up_field(last), 0:frames, 1 : rows + 1], 0)
    for layer in reversed(range(blocks)):
        load(("in", layer), block_in.at[layer], fields.at[layer, 2 : frames + 2, 1 : rows + 1], 1 + layer)
        load(("w1", layer), w1_hbm.at[layer], w1.at[layer], 1 + blocks + layer)
        load(("w2", layer), w2_hbm.at[layer], w2.at[layer], 1 + 2 * blocks + layer)

    barrier = pltpu.get_barrier_semaphore()

    def greet(dtm, to):
        pl.semaphore_signal(
            barrier, inc=1, device_id={"tm": tm + dtm, "space": to},
            device_id_type=pl.DeviceIdType.MESH,
        )

    for k in range(1, n_sp):
        greet(0, lax.rem(sp + k, n_sp))
    expected = n_sp - 1
    for dtm, can in ((1, after), (-1, before)):
        pl.when(can)(functools.partial(greet, dtm, sp))
        expected = expected + jnp.where(can, 1, 0)

    pair_range = range(pairs)

    at_col = lax.broadcasted_iota(jnp.int32, (cols, chan), 0)

    def spread(x, frame, row, value):
        wide = value.astype(F32)
        left = jnp.where(at_col == 0, 0.0, pltpu.roll(wide, 1, axis=0))
        right = jnp.where(at_col == cols - 1, 0.0, pltpu.roll(wide, cols - 1, axis=0))
        x[frame, row, :, 0:chan] = left.astype(BF16)
        x[frame, row, :, chan : 2 * chan] = value
        x[frame, row, :, 2 * chan : 3 * chan] = right.astype(BF16)

    def clear(x, frame, row):
        x[frame, row] = jnp.zeros((cols, 3 * chan), BF16)

    def edge(x, field, frame, row, present):
        @pl.when(present)
        def _():
            spread(x, frame, row, fields[field, frame, row])

        @pl.when(jnp.logical_not(present))
        def _():
            clear(x, frame, row)

    def row_edges(x, field, past, pair):
        arrive(row_copies(field, past, pair))
        for i in range(2):
            frame = 2 * pair + i + (2 if past else 0)
            edge(x, field, frame, 0, low)
            edge(x, field, frame, rows + 1, high)

    def accept(field, past):
        arrive(time_copies(field, past))
        start(corner_copies(field, past))

    def time_edges(x, field, past):
        present = before if past else after
        for i in range(2):
            frame = i if past else frames + i

            @pl.when(present)
            def _():
                @pl.loop(1, rows + 1)
                def _(row):
                    spread(x, frame, row, fields[field, frame, row])

            @pl.when(jnp.logical_not(present))
            def _():
                @pl.loop(1, rows + 1)
                def _(row):
                    clear(x, frame, row)

        arrive(corner_copies(field, past))
        for i in range(2):
            frame = i if past else frames + i
            edge(x, field, frame, 0, present & low)
            edge(x, field, frame, rows + 1, present & high)

    def own_rows(x, field, past):
        @pl.loop(0, frames * rows)
        def _(at):
            frame = at // rows + (2 if past else 0)
            row = at % rows + 1
            spread(x, frame, row, fields[field, frame, row])

    def tap(w, layer, a, flip):
        if not flip:
            return w[layer, a].reshape(9 * chan, chan)
        return jnp.concatenate([w[layer, a, 2 - r, 2 - s] for r in range(3) for s in range(3)], axis=1)

    def conv(acc, x, w, layer, flip, pair, order, hooks):
        zero = jnp.zeros((chan, 9 * chan) if flip else (9 * chan, chan), BF16)
        outer = 0 if flip else 1

        def part(j, r, half):
            first = r + half * rows // 2
            return x[2 * pair + j, first : first + rows // 2].reshape(pixels // 2, 3 * chan)

        for step, group_of in enumerate(order):
            rhs = []
            for j in group_of:
                if j in hooks:
                    hooks[j]()
            for j in group_of:
                taps = [(2 - k if flip else k) if 0 <= k <= 2 else None for k in (j, j - 1)]
                parts = [zero if a is None else tap(w, layer, a, flip) for a in taps]
                rhs.append(jnp.concatenate(parts, axis=outer))
            right = jnp.concatenate(rhs, axis=1 if flip else 0)
            dims = (((1,), (1,)), ((), ())) if flip else (((1,), (0,)), ((), ()))
            for half in range(2):
                at = slice(half * pixels // 2, (half + 1) * pixels // 2)
                left = jnp.concatenate([part(j, r, half) for j in group_of for r in range(3)], axis=1)
                value = lax.dot_general(left, right, dims, preferred_element_type=F32)
                if step == 0:
                    acc[at] = value
                else:
                    acc[at] += value

    def conv_past(layer, pair):
        order, hooks = ((0, 1), (2, 3)), {}
        if pair == 0:
            order, hooks = ((2, 3), (0, 1)), {0: lambda: time_edges(x_past, layer, True)}
        conv(pre_acc.at[layer, pair], x_past, w1, layer, False, pair, order, hooks)

    def conv_future(x, w, layer, field, pair):
        hooks = {}
        if pair == 0:
            hooks[0] = lambda: row_edges(x, field, False, 0)
        if pair < pairs - 1:
            hooks[2] = lambda: row_edges(x, field, False, pair + 1)
        else:
            hooks[2] = lambda: time_edges(x, field, False)
        conv(grad_acc.at[pair], x, w, layer, True, pair, ((0, 1), (2, 3)), hooks)

    def make(field, pair, each):
        for i in range(2):
            for row in (0, rows - 1):
                each(i, row)
        start(row_copies(field, False, pair))
        for i in range(2):
            pl.loop(1, rows - 1, unroll=2)(functools.partial(each, i))
        if pair == 0:
            start(time_copies(field, False))

    def place(row):
        return pl.ds(pl.multiple_of(row * cols, cols), cols)

    pl.semaphore_wait(barrier, expected)
    start(time_copies(last, True))
    for layer in reversed(range(blocks)):
        for pair in reversed(pair_range):
            start(row_copies(layer, True, pair))

    def scaled(pair):
        def each(i, row):
            frame = 2 * pair + i
            scale = adv[group[frame]]
            value = (fields[up_field(last), frame, row + 1].astype(F32) * scale).astype(BF16)
            fields[up_field(last), frame, row + 1] = value
            spread(x_up, frame, row + 1, value)

        make(up_field(last), pair, each)

    loads["cot"].wait()
    for pair in pair_range:
        scaled(pair)

    def grad_pre(layer, pair):
        field = gr_field(layer)

        def each(i, row):
            at = place(row)
            lanes = slice(i * chan, (i + 1) * chan)
            grad = grad_acc[pair, at, lanes]
            pre = pre_acc[layer, pair, at, lanes]
            s = jax.nn.sigmoid(pre)
            value = (grad * (s * (1.0 + pre * (1.0 - s)))).astype(BF16)
            fields[field, 2 * pair + i, row + 1] = value
            spread(x_gr, 2 * pair + i, row + 1, value)

        make(field, pair, each)

    def next_up(layer, pair):
        field = up_field(layer - 1)

        def each(i, row):
            back = grad_acc[pair, place(row), i * chan : (i + 1) * chan]
            value = (fields[up_field(layer), 2 * pair + i, row + 1].astype(F32) + back).astype(BF16)
            fields[field, 2 * pair + i, row + 1] = value
            spread(x_up, 2 * pair + i, row + 1, value)

        make(field, pair, each)

    def pool(layer, pair):
        for i in range(2):
            @pl.loop(0, rows // 2)
            def _(r):
                total = jnp.zeros((cols, chan), F32)
                for k in range(2):
                    row = 2 * r + k
                    at = pl.ds(pl.multiple_of(row * cols, cols), cols)
                    back = grad_acc[pair, at, i * chan : (i + 1) * chan]
                    value = fields[up_field(layer), 2 * pair + i, row + 1].astype(F32) + back
                    total = total + value.astype(BF16).astype(F32)
                at = pl.multiple_of(((2 * pair + i) * (rows // 2) + r) * cols, cols)
                pool_a[pl.ds(at, cols), :] = total

    def past_ahead(layer):
        loads[("in", layer)].wait()
        own_rows(x_past, layer, True)
        for pair in reversed(pair_range):
            row_edges(x_past, layer, True, pair)
        loads[("w1", layer)].wait()
        for pair in reversed(range(1, pairs)):
            conv_past(layer, pair)

    past_ahead(last)
    for layer in reversed(range(blocks)):
        up, gr = up_field(layer), gr_field(layer)
        loads[("w2", layer)].wait()
        if layer < last:
            accept(layer, True)
        conv_future(x_up, w2, layer, up, 0)
        if layer == last:
            accept(layer, True)
        conv_past(layer, 0)
        grad_pre(layer, 0)
        if layer > 0:
            start(time_copies(layer - 1, True))
            past_ahead(layer - 1)
        for pair in range(1, pairs):
            if pair == pairs - 1:
                accept(up, False)
            conv_future(x_up, w2, layer, up, pair)
            grad_pre(layer, pair)
        for pair in pair_range:
            if pair == pairs - 1:
                accept(gr, False)
            conv_future(x_gr, w1, layer, gr, pair)
            if layer > 0:
                next_up(layer, pair)
            else:
                pool(layer, pair)

    units_n = owner.shape[1]
    cap = out.shape[3]
    places = n_sp * cap
    lat = pool_b.shape[0]
    even = pool_a[pl.ds(0, lat, stride=2), :]
    odd = pool_a[pl.ds(1, lat, stride=2), :]
    pool_b[...] = (even + odd).astype(BF16).astype(F32)
    wide = lat // units_n
    units = jnp.concatenate(
        [pool_b[pl.ds(k, units_n, stride=wide), :] for k in range(wide)], axis=1
    ).astype(BF16)
    owners = owner[...]
    hot = jnp.where(owners == lax.broadcasted_iota(jnp.int32, (128, units_n), 0), 1.0, 0.0)
    tri = jnp.where(
        lax.broadcasted_iota(jnp.int32, (units_n, units_n), 0)
        <= lax.broadcasted_iota(jnp.int32, (units_n, units_n), 1), 1.0, 0.0,
    )
    ranks = jnp.dot(hot.astype(BF16), tri.astype(BF16), preferred_element_type=F32)
    position = jnp.sum(ranks * hot, axis=0, keepdims=True) - 1.0
    slot = owners.astype(F32) * cap + position
    chosen = jnp.where(
        slot == lax.broadcasted_iota(jnp.int32, (places, units_n), 0).astype(F32), 1.0, 0.0
    )
    placed = jnp.dot(chosen.astype(BF16), units, preferred_element_type=F32)
    for o in range(n_sp):
        outgoing[o] = placed[o * cap : (o + 1) * cap].astype(BF16)

    mine = pltpu.make_async_copy(outgoing.at[sp], out.at[0, 0, sp], local_sem.at[1 + 3 * blocks])
    mine.start()
    moves = []
    for k in range(1, n_sp):
        to = lax.rem(sp + k, n_sp)
        copy = pltpu.make_async_remote_copy(
            src_ref=outgoing.at[to], dst_ref=out.at[0, 0, sp],
            send_sem=a2a_send.at[k], recv_sem=a2a_recv.at[k],
            device_id={"space": to}, device_id_type=pl.DeviceIdType.MESH,
        )
        copy.start()
        moves.append(copy)
    mine.wait()
    for k, copy in enumerate(moves, 1):
        copy.wait_send()
        came = lax.rem(sp - k + n_sp, n_sp)
        pltpu.make_async_remote_copy(
            src_ref=outgoing.at[came], dst_ref=out.at[0, 0, came],
            send_sem=a2a_send.at[k], recv_sem=a2a_recv.at[k],
            device_id={"space": came}, device_id_type=pl.DeviceIdType.MESH,
        ).wait_recv()
    for layer in range(blocks):
        sent(time_copies(layer, True))
        sent(corner_copies(layer, True))
        for field in (up_field(layer), gr_field(layer)):
            sent(time_copies(field, False))
            sent(corner_copies(field, False))
        for pair in pair_range:
            sent(row_copies(layer, True, pair))
            for field in (up_field(layer), gr_field(layer)):
                sent(row_copies(field, False, pair))


def on_device(pixel_cot, frame_group, advantage, block_in, conv1_weight, conv2_weight, owner_map):
    frames, rows, cols, chan = pixel_cot.shape
    blocks = block_in.shape[0]
    pairs = frames // 2
    units = owner_map.shape[2]
    n_sp = lax.axis_size("space")
    cap = max(2, 2 * units // n_sp)
    unit = frames * (rows // 2) * (cols // 2) * chan // units
    lat = frames * (rows // 2) * (cols // 2)
    spread = (frames + 2, rows + 2, cols, 3 * chan)
    smem = pl.BlockSpec(memory_space=pltpu.SMEM)
    hbm = pl.BlockSpec(memory_space=pl.ANY)
    vmem = pl.BlockSpec(memory_space=pltpu.VMEM)
    return pl.pallas_call(
        kernel,
        out_shape=jax.ShapeDtypeStruct((1, 1, n_sp, cap, unit), BF16),
        in_specs=[hbm, smem, smem, hbm, hbm, hbm, vmem],
        out_specs=hbm,
        scratch_shapes=[
            pltpu.VMEM(conv1_weight.shape, BF16),
            pltpu.VMEM(conv2_weight.shape, BF16),
            pltpu.VMEM((3 * blocks, frames + 2, rows + 2, cols, chan), BF16),
            pltpu.VMEM(spread, BF16),
            pltpu.VMEM(spread, BF16),
            pltpu.VMEM(spread, BF16),
            pltpu.VMEM((blocks, pairs, rows * cols, 2 * chan), F32),
            pltpu.VMEM((pairs, rows * cols, 2 * chan), F32),
            pltpu.VMEM((2 * lat, chan), F32),
            pltpu.VMEM((lat, chan), F32),
            pltpu.VMEM((n_sp, cap, unit), BF16),
            pltpu.SemaphoreType.DMA((3 * blocks, 3 + 2 * pairs)),
            pltpu.SemaphoreType.DMA((3 * blocks, 3 + 2 * pairs)),
            pltpu.SemaphoreType.DMA((n_sp,)),
            pltpu.SemaphoreType.DMA((n_sp,)),
            pltpu.SemaphoreType.DMA((2 + 3 * blocks,)),
        ],
        compiler_params=pltpu.CompilerParams(
            has_side_effects=True, collective_id=0, vmem_limit_bytes=60 * 1024 * 1024
        ),
    )(pixel_cot, frame_group, advantage, block_in, conv1_weight, conv2_weight, owner_map.reshape(1, units))


def solution(mesh):
    in_specs = (
        P("tm", "space", None, None),
        P("tm"),
        P(),
        P(None, "tm", "space", None, None),
        P(),
        P(),
        P("tm", "space", None, None),
    )
    out_specs = P("tm", "space", None, None, None)
    return jax.shard_map(
        on_device, mesh=mesh, in_specs=in_specs, out_specs=out_specs, check_vma=False
    )
```
